768 devices in a mesh: span: 12 (over z), shard: 64 (over x, y, core).
Axes of the slice: x: 4, y: 8, z: 12, core: 2. Of those that a mesh axis runs over, the one named last changes fastest.
Arguments:
- tokens: bfloat16 [196608, 1152], P(('span', 'shard')), may hold values from -6 to 6
- out_proj: bfloat16 [1152, 1152], replicated, may hold values from -0.1875 to 0.1875
- phi_mean: float32 [1152], replicated, may hold values from -6 to 6
- phi_rotate: bfloat16 [1152, 576], replicated, may hold values from -0.1875 to 0.1875
- destinations: int32 [196608, 1], P(('span', 'shard')), may hold values from 0 to 11; in each aligned block of 256 rows (0 to 255, 256 to 511, ...) at most 32 rows name the same one
- student_hidden: bfloat16 [294912, 1280], P(('span', 'shard')), may hold values from -6 to 6
- adaptor: bfloat16 [1280, 576], replicated, may hold values from -0.15625 to 0.15625
- master: float32 [1280, 576], P('shard'), may hold values from -0.15625 to 0.15625
- moment_one: float32 [1280, 576], P('shard'), may hold values from -4 to 4
- moment_two: float32 [1280, 576], P('shard'), may hold values from 0.01 to 1
Outputs:
- updated_master: float32 [1280, 576], P('shard')
- updated_first: float32 [1280, 576], P('shard')
- updated_second: float32 [1280, 576], P('shard')
The draws below stay inside these ranges and needn't reach their ends.
Inputs may be any that keep to these rules, and one draw needn't show every extreme that they name: `destinations`: at most 32 of the 256 rows of one device name one span; some span gets exactly 32.
All inputs are finite; a program needn't handle non-finite values.
Results may differ from the reference program's by a relative error of at most 0.00064.
Values may be sent and summed in bfloat16 or wider, within the bound.
No kernel may reach another device: no remote copies, remote signals or barrier semaphores. Data moves between devices by JAX's collectives and lax.ppermute only.
A program may use at most 64 MiB of HBM per device.

```python
import math
import jax
import jax.numpy as jnp
import numpy as np
from jax import lax

DT = 1152
DW = 576
H = 1280
ROWS_DEV = 256
ADAM_STEP = 1000
CAP = 32
SLOTS = 384
TEACH_ROWS = 196608
STUD_SLOTS = 294912
N_SPAN = 12
N_SHARD = 64


def levels(stream_key, shape, split, low, high):
    level = 1.0
    for position, blocks in split:
        steps = jax.random.uniform(jax.random.fold_in(jax.random.fold_in(stream_key, 6), position), (blocks,), jnp.float32, low / len(split), high / len(split))
        level = level * jnp.repeat(jnp.exp(steps), shape[position] // blocks).reshape((-1,) + (1,) * (len(shape) - 1 - position))
    return level


def shared_out(key, own, number, rows, number_of, top, most, lean):
    sequence = jax.random.permutation(key, number_of)
    heavy_load, common = load_shares(number_of, rows * top, most, lean, True), load_shares(number_of, rows * top, most, lean, False)
    places = jnp.arange(number_of)

    def named(lengths, offset_by):
        used = int((lengths > 0).sum())
        fixed = max(1, used // 4)
        passed = fixed + (places - fixed + offset_by * (used - fixed)) % max(1, number_of - fixed)
        return jnp.zeros((number_of,), jnp.int32).at[sequence[jnp.where(places < fixed, places, passed)]].set(jnp.asarray(lengths, jnp.int32))

    lengths = jnp.where(number % 4 == 0, named(heavy_load, number // 4), named(common, number - number // 4 - 1))
    mixed = jax.random.permutation(jax.random.fold_in(own, 3), number_of)
    giver, taker = mixed[0:number_of // 2 * 2:2], mixed[1:number_of // 2 * 2:2]
    margin = jnp.minimum(lengths[giver] - 1, most - lengths[taker]) // 2
    margin = jnp.where((giver == sequence[0]) | (taker == sequence[0]) | (lengths[taker] == 0), 0, jnp.maximum(margin, 0))
    passed = jax.random.randint(jax.random.fold_in(own, 4), (number_of // 2,), 0, 1 << 20) % (margin + 1)
    lengths = lengths.at[giver].add(-passed).at[taker].add(passed)
    labels = jnp.searchsorted(jnp.cumsum(lengths), jnp.arange(rows * top), side="right").astype(jnp.int32)
    table = labels.reshape(top, rows).T
    table = table[jax.random.permutation(jax.random.fold_in(own, 1), rows)]
    offset_by = jax.random.randint(jax.random.fold_in(own, 2), (rows, 1), 0, top)
    return jnp.take_along_axis(table, (jnp.arange(top)[None, :] + offset_by) % top, axis=1)


def load_shares(count, total, reach, skew, full):
    loads = [(1 << 20) // math.isqrt(standing ** skew) + 1 for standing in range(1, count + 1)]
    largest = reach if full else min(reach, max(-(-total // count), total * loads[0] // sum(loads)))
    least = 1 if total - largest >= count - 1 else 0
    given, spare = [largest] + [least] * (count - 1), total - largest - least * (count - 1)
    while spare > 0:
        free = [i for i in range(1, count) if given[i] < largest] or [i for i in range(1, count) if given[i] < reach]
        mass, budget = sum([loads[i] for i in free]), spare
        for i in free:
            addition = min(reach - given[i], max(1, budget * loads[i] // mass), spare)
            given[i] = given[i] + addition
            spare = spare - addition
    return np.array(given)


def noise(rng, extent, spread, reach, shards=(), kind=jnp.bfloat16):
    level = levels(rng, extent, shards, -0.22, 0.18) if shards else 1.0
    values = jax.random.normal(rng, extent, jnp.float32) * spread * level
    return jnp.minimum(jnp.maximum(values, -reach), reach).astype(kind)


def setup_inputs(seed: int = 0) -> dict:
    key_of = jax.random.split(jax.random.key(seed), 11)
    tokens = noise(key_of[0], (TEACH_ROWS, DT), 1.0, 6.0, ((0, 768),))
    out_proj = noise(key_of[1], (DT, DT), DT ** -0.5, 0.1875)
    phi_mean = noise(key_of[2], (DT,), 1.0, 6.0, (), jnp.float32)
    phi_rotate = noise(key_of[3], (DT, DW), DT ** -0.5, 0.1875)
    destinations_keys = jax.random.split(jax.random.fold_in(key_of[4], 1), TEACH_ROWS // ROWS_DEV)
    destinations_turns = jax.random.permutation(jax.random.fold_in(key_of[4], 3), TEACH_ROWS // ROWS_DEV)
    destinations = jax.vmap(lambda own, number: shared_out(jax.random.fold_in(key_of[4], 2), own, number, ROWS_DEV, N_SPAN, 1, CAP, 2))(destinations_keys, destinations_turns).reshape((TEACH_ROWS, 1))
    student_hidden = noise(key_of[5], (STUD_SLOTS, H), 1.0, 6.0, ((0, 768),))
    adaptor = noise(key_of[6], (H, DW), H ** -0.5, 0.15625)
    master = noise(key_of[7], (H, DW), H ** -0.5, 0.15625, ((0, 64),), jnp.float32)
    moment_one = noise(key_of[8], (H, DW), 0.3, 4.0, ((0, 64),), jnp.float32)
    moment_two = jnp.clip(jnp.exp(math.log(1.0) - 4.6051702 * jax.random.uniform(key_of[9], (H, DW), jnp.float32) ** levels(key_of[9], (H, DW), ((0, 64),), -0.2, 0.2)), 0.01, 1.0)
    return {"tokens": tokens, "out_proj": out_proj, "phi_mean": phi_mean, "phi_rotate": phi_rotate, "destinations": destinations, "student_hidden": student_hidden, "adaptor": adaptor, "master": master, "moment_one": moment_one, "moment_two": moment_two}


beta_first = 0.9
beta_second = 0.999
adam_epsilon = 1e-08
decay_rate = 0.05
learn_rate = 0.001

def reference(tokens, out_proj, phi_mean, phi_rotate, destinations, student_hidden, adaptor, master, moment_one, moment_two):
    span_count = N_SPAN
    shard_count = N_SHARD
    target_span = destinations[:, 0].reshape(span_count, shard_count, ROWS_DEV)
    span_ids = jnp.arange(span_count, dtype=jnp.int32)
    one_hot = (target_span[..., None] == span_ids).astype(jnp.int32)
    slot_rank = lax.optimization_barrier(jnp.sum((jnp.cumsum(one_hot, axis=2) - one_hot) * one_hot, axis=3))
    source = span_ids[:, None, None]
    shard_ids = jnp.arange(shard_count, dtype=jnp.int32)[None, :, None]
    placement_ids = ((target_span * shard_count + shard_ids) * SLOTS + source * CAP + slot_rank).astype(jnp.int32)
    token_blocks = tokens.reshape(span_count, shard_count * ROWS_DEV, DT)
    place_blocks = placement_ids.reshape(span_count, shard_count * ROWS_DEV)

    def one_span(running, paired):
        block_rows, block_place = paired
        projected = (jnp.dot(block_rows, out_proj, preferred_element_type=jnp.float32) - phi_mean).astype(jnp.bfloat16)
        target = jnp.dot(projected, phi_rotate, preferred_element_type=jnp.float32).astype(jnp.bfloat16)
        hidden = student_hidden[block_place]
        activated = jax.nn.gelu(hidden.astype(jnp.float32), approximate=False).astype(jnp.bfloat16)
        predicted = jnp.dot(activated, adaptor, preferred_element_type=jnp.float32)
        scaled_error = ((predicted - target.astype(jnp.float32)) / DW).astype(jnp.bfloat16)
        return (running + jnp.dot(activated.T, scaled_error, preferred_element_type=jnp.float32), None)
    gradient, unused = lax.scan(one_span, jnp.zeros((H, DW), jnp.float32), (token_blocks, place_blocks))
    first_new = beta_first * moment_one + (1.0 - beta_first) * gradient
    second_new = beta_second * moment_two + (1.0 - beta_second) * gradient * gradient
    bias_first = 1.0 - beta_first ** ADAM_STEP
    bias_second = 1.0 - beta_second ** ADAM_STEP
    update_dir = first_new / bias_first / (jnp.sqrt(second_new / bias_second) + adam_epsilon) + decay_rate * master
    return (master - learn_rate * update_dir, first_new, second_new)
```

```python
import functools

import jax
import jax.numpy as jnp
from jax import lax
from jax.experimental import pallas as pl
from jax.experimental.pallas import tpu as pltpu
from jax.sharding import Mesh, PartitionSpec as P

ADAM_STEP = 1000
beta_first = 0.9
beta_second = 0.999
adam_epsilon = 1e-08
decay_rate = 0.05
learn_rate = 0.001

NZ, NX, NY, NC = 12, 4, 8, 2
CAP = 32
ROWS = 256
SLOTS = NZ * CAP
H = 1280
DW = 576
WIDE = 640
OWN = H // (NX * NY * NC)
HALF = H // NC
XB = HALF // NX
TILE_ROWS = NZ * 8
f32 = jnp.float32
bf16 = jnp.bfloat16
YZ_TYPE = bf16


def call(kernel, outs, args, scratch=(), vmem=24, specs=None, flops=0, moved=0):
    return pl.pallas_call(
        kernel,
        out_shape=outs,
        in_specs=specs or [pl.BlockSpec()] * len(args),
        scratch_shapes=list(scratch),
        compiler_params=pltpu.CompilerParams(vmem_limit_bytes=vmem * 2**20),
        cost_estimate=pl.CostEstimate(flops=flops, bytes_accessed=moved, transcendentals=0),
    )(*args)


def route_kernel(dest_ref, rows_ref, out_ref):
    dest = dest_ref[...]
    spans = lax.broadcasted_iota(jnp.int32, (16, ROWS), 0)
    named = spans == dest
    one_hot = jnp.where(named, 1.0, 0.0)
    earlier = (
        lax.broadcasted_iota(jnp.int32, (ROWS, ROWS), 0)
        < lax.broadcasted_iota(jnp.int32, (ROWS, ROWS), 1)
    )
    before = jnp.dot(
        one_hot.astype(bf16),
        jnp.where(earlier, 1.0, 0.0).astype(bf16),
        preferred_element_type=f32,
    )
    rank = jnp.sum(before * one_hot, axis=0, keepdims=True)
    slot = dest * CAP + rank.astype(jnp.int32)
    place = lax.broadcasted_iota(jnp.int32, (SLOTS, ROWS), 0) == slot
    out_ref[...] = jnp.dot(
        jnp.where(place, 1.0, 0.0).astype(bf16), rows_ref[...], preferred_element_type=f32
    ).astype(bf16)


def student_kernel(core_ref, act_ref, adaptor_t_ref, pred_ref, send_ref, keep_ref):
    nt = (((1,), (1,)), ((), ()))
    act = act_ref[...]
    pred_ref[...] = lax.dot_general(act, adaptor_t_ref[...], nt, preferred_element_type=f32)
    core = core_ref[0]
    place = lax.broadcasted_iota(jnp.int32, (HALF, 1), 0)
    unit = place + OWN * (place // OWN)
    column = lax.broadcasted_iota(jnp.int32, (HALF, H), 1)
    for ref, owner in ((send_ref, 1 - core), (keep_ref, core)):
        pick = jnp.where(column == unit + OWN * owner, 1.0, 0.0).astype(bf16)
        ref[...] = lax.dot_general(pick, act, nt, preferred_element_type=f32).astype(bf16)


def error_kernel(arrived_ref, pred_ref, send_ref, error_ref, out_ref):
    live = arrived_ref[:, DW : DW + 1].astype(f32) > 0.5
    error = jnp.where(live, pred_ref[...] - arrived_ref[:, :DW].astype(f32), 0.0)
    error = (error / DW).astype(bf16)
    error_ref[...] = error
    out_ref[:, :DW] = jnp.dot(send_ref[...], error, preferred_element_type=f32).astype(bf16)
    out_ref[:, DW:] = jnp.zeros((HALF, WIDE - DW), bf16)


def keep_kernel(keep_ref, error_ref, out_ref):
    out_ref[...] = jnp.dot(keep_ref[...], error_ref[...], preferred_element_type=f32)


def add_kernel(own_ref, got_ref, out_ref):
    out_ref[...] = (own_ref[...] + got_ref[:, :DW].astype(f32)).astype(bf16)


def tile_kernel(got_ref, out_ref, sum_ref, flat_ref):
    total = got_ref[0].astype(f32)
    for x in range(1, NX):
        total = total + got_ref[x].astype(f32)
    sum_ref[:, :DW] = total
    sum_ref[:, DW:] = jnp.zeros((XB, WIDE - DW), f32)
    left = lax.broadcasted_iota(jnp.int32, (OWN // 2, 128), 1) < 64
    for y in range(NY):
        at, to = y * OWN, y * TILE_ROWS
        for l in range(4):
            flat_ref[to + l * OWN : to + (l + 1) * OWN, :] = sum_ref[
                at : at + OWN, l * 128 : (l + 1) * 128
            ]
        upper = sum_ref[at : at + OWN // 2, 512:640]
        lower = pltpu.roll(sum_ref[at + OWN // 2 : at + OWN, 512:640], 64, axis=1)
        flat_ref[to + 80 : to + 90, :] = jnp.where(left, upper, lower)
        flat_ref[to + 90 : to + 96, :] = jnp.zeros((6, 128), f32)
        for z in range(NZ):
            out_ref[z * NY + y] = flat_ref[to + z * 8 : to + z * 8 + 8, :].astype(out_ref.dtype)


def adam_kernel(tiles_ref, master_ref, one_ref, two_ref, m_out, f_out, s_out, grad_ref):
    for l in range(4):
        grad_ref[:, l * 128 : (l + 1) * 128] = tiles_ref[l * OWN : (l + 1) * OWN, :]
    last = tiles_ref[80:90, :]
    grad_ref[0:10, 512:640] = last
    grad_ref[10:20, 512:640] = pltpu.roll(last, 64, axis=1)
    gradient = grad_ref[:, :DW]
    master = master_ref[...]
    first_new = beta_first * one_ref[...] + (1.0 - beta_first) * gradient
    second_new = beta_second * two_ref[...] + (1.0 - beta_second) * gradient * gradient
    bias_first = 1.0 - beta_first**ADAM_STEP
    bias_second = 1.0 - beta_second**ADAM_STEP
    update_dir = (
        first_new / bias_first / (jnp.sqrt(second_new / bias_second) + adam_epsilon)
        + decay_rate * master
    )
    m_out[...] = master - learn_rate * update_dir
    f_out[...] = first_new
    s_out[...] = second_new


def exchange(x, axis):
    return lax.all_to_all(x, axis, split_axis=0, concat_axis=0, tiled=True)


def body(
    tokens,
    out_proj,
    phi_mean,
    phi_rotate,
    destinations,
    student_hidden,
    adaptor,
    master,
    moment_one,
    moment_two,
):
    shape = jax.ShapeDtypeStruct
    projected = (jnp.dot(tokens, out_proj, preferred_element_type=f32) - phi_mean).astype(bf16)
    target = jnp.dot(projected, phi_rotate, preferred_element_type=f32).astype(bf16)
    marked = jnp.pad(target, ((0, 0), (0, WIDE - DW)), constant_values=1.0)
    outgoing = call(
        route_kernel,
        shape((SLOTS, WIDE), bf16),
        (destinations.reshape(1, ROWS), marked),
        flops=2 * SLOTS * ROWS * WIDE,
        moved=2 * WIDE * (SLOTS + ROWS),
    )
    arrived = exchange(outgoing.reshape(NZ, CAP, WIDE), "z").reshape(SLOTS, WIDE)

    activated = jax.nn.gelu(student_hidden.astype(f32), approximate=False).astype(bf16)
    core = lax.axis_index("c").astype(jnp.int32).reshape(1)
    whole = pl.BlockSpec()
    predicted, act_send, act_keep = call(
        student_kernel,
        (shape((SLOTS, DW), f32), shape((HALF, SLOTS), bf16), shape((HALF, SLOTS), bf16)),
        (core, activated, adaptor.T),
        specs=[pl.BlockSpec(memory_space=pltpu.SMEM), whole, whole],
        flops=2 * SLOTS * H * (DW + H),
        moved=2 * SLOTS * H * 2 + 2 * H * DW + 4 * SLOTS * DW,
    )
    error, for_partner = call(
        error_kernel,
        (shape((SLOTS, DW), bf16), shape((HALF, WIDE), bf16)),
        (arrived, predicted, act_send),
        flops=2 * SLOTS * HALF * DW,
        moved=2 * SLOTS * (WIDE + 3 * DW + HALF) + 2 * HALF * DW,
    )
    from_partner = lax.ppermute(for_partner, "c", [(0, 1), (1, 0)])
    own = call(
        keep_kernel,
        shape((HALF, DW), f32),
        (act_keep, error),
        flops=2 * SLOTS * HALF * DW,
        moved=2 * SLOTS * (DW + HALF) + 4 * HALF * DW,
    )
    chip_sum = call(
        add_kernel, shape((HALF, DW), bf16), (own, from_partner), moved=8 * HALF * DW
    )
    by_x = exchange(chip_sum.reshape(NX, XB, DW), "x")
    tiles = call(
        tile_kernel,
        shape((NZ * NY, 8, 128), YZ_TYPE),
        (by_x,),
        scratch=(pltpu.VMEM((XB, WIDE), f32), pltpu.VMEM((NY * TILE_ROWS, 128), f32)),
        moved=4 * XB * DW * 4,
    )
    by_yz = exchange(tiles, ("z", "y"))
    part = by_yz.astype(f32).sum(axis=0)
    gathered = exchange(jnp.broadcast_to(part, (NZ, 8, 128)), "z").reshape(TILE_ROWS, 128)
    out = shape((OWN, DW), f32)
    return call(
        adam_kernel,
        (out, out, out),
        (gathered, master, moment_one, moment_two),
        scratch=(pltpu.VMEM((OWN, WIDE), f32),),
        moved=4 * OWN * DW * 7,
    )


def solution(mesh):
    grid = Mesh(mesh.devices.reshape(NZ, NX, NY, NC), ("z", "x", "y", "c"))
    shard = ("x", "y", "c")
    rows = P(("z", "x", "y", "c"), None)
    state = P(shard, None)
    in_specs = (rows, P(), P(), P(), rows, rows, P(), state, state, state)
    return jax.shard_map(
        body, mesh=grid, in_specs=in_specs, out_specs=(state, state, state), check_vma=False
    )
```

```python
import functools

import jax
import jax.numpy as jnp
from jax import lax
from jax.experimental import pallas as pl
from jax.experimental.pallas import tpu as pltpu
from jax.sharding import Mesh, PartitionSpec as P

ADAM_STEP = 1000
beta_first = 0.9
beta_second = 0.999
adam_epsilon = 1e-08
decay_rate = 0.05
learn_rate = 0.001

NZ, NX, NY, NC = 12, 4, 8, 2
CAP = 32
ROWS = 256
SLOTS = NZ * CAP
H = 1280
DW = 576
WIDE = 640
OWN = H // (NX * NY * NC)
HALF = H // NC
XB = HALF // NX
TILE_ROWS = NZ * 8
DT = 1152
STEPS = 3
CHUNK = DT // STEPS
f32 = jnp.float32
bf16 = jnp.bfloat16
Y_TYPE = bf16


def call(kernel, outs, args, scratch=(), vmem=24, specs=None, flops=0, moved=0, **kinds):
    return pl.pallas_call(
        kernel,
        out_shape=outs,
        in_specs=specs or [pl.BlockSpec()] * len(args),
        **kinds,
        scratch_shapes=list(scratch),
        compiler_params=pltpu.CompilerParams(vmem_limit_bytes=vmem * 2**20),
        cost_estimate=pl.CostEstimate(flops=flops, bytes_accessed=moved, transcendentals=0),
    )(*args)


def teacher_kernel(
    dest_ref,
    mean_ref,
    tokens_hbm,
    proj_hbm,
    rotate_hbm,
    out_ref,
    tokens_ref,
    proj_ref,
    rotate_ref,
    rows_ref,
    token_sem,
    proj_sems,
    rotate_sems,
):
    token_copy = pltpu.make_async_copy(tokens_hbm, tokens_ref, token_sem)
    token_copy.start()
    copies = []
    for k in range(STEPS):
        part = pl.ds(k * CHUNK, CHUNK)
        pair = (
            pltpu.make_async_copy(proj_hbm.at[:, part], proj_ref.at[k], proj_sems.at[k]),
            pltpu.make_async_copy(rotate_hbm.at[:, part], rotate_ref.at[k], rotate_sems.at[k]),
        )
        for copy in pair:
            copy.start()
        copies.append(pair)

    dest = dest_ref[...]
    spans = lax.broadcasted_iota(jnp.int32, (16, ROWS), 0)
    one_hot = jnp.where(spans == dest, 1.0, 0.0)
    earlier = (
        lax.broadcasted_iota(jnp.int32, (ROWS, ROWS), 0)
        < lax.broadcasted_iota(jnp.int32, (ROWS, ROWS), 1)
    )
    before = jnp.dot(
        one_hot.astype(bf16),
        jnp.where(earlier, 1.0, 0.0).astype(bf16),
        preferred_element_type=f32,
    )
    rank = jnp.sum(before * one_hot, axis=0, keepdims=True)
    slot = dest * CAP + rank.astype(jnp.int32)
    rows_ref[:, DW:] = jnp.ones((ROWS, WIDE - DW), bf16)

    token_copy.wait()
    tokens = tokens_ref[...]
    total = None
    for k, (proj_copy, rotate_copy) in enumerate(copies):
        proj_copy.wait()
        projected = jnp.dot(tokens, proj_ref[k], preferred_element_type=f32)
        projected = (projected - mean_ref[:, k * CHUNK : (k + 1) * CHUNK]).astype(bf16)
        rotate_copy.wait()
        part = lax.dot_general(
            projected, rotate_ref[k], (((1,), (1,)), ((), ())), preferred_element_type=f32
        )
        total = part if total is None else total + part
    rows_ref[:, :DW] = total.astype(bf16)
    place = lax.broadcasted_iota(jnp.int32, (SLOTS, ROWS), 0) == slot
    out_ref[...] = jnp.dot(
        jnp.where(place, 1.0, 0.0).astype(bf16), rows_ref[...], preferred_element_type=f32
    ).astype(bf16)


def student_kernel(core_ref, act_ref, adaptor_t_ref, pred_ref, send_ref, keep_ref):
    nt = (((1,), (1,)), ((), ()))
    act = act_ref[...]
    pred_ref[...] = lax.dot_general(act, adaptor_t_ref[...], nt, preferred_element_type=f32)
    core = core_ref[0]
    place = lax.broadcasted_iota(jnp.int32, (HALF, 1), 0)
    unit = place + OWN * (place // OWN)
    column = lax.broadcasted_iota(jnp.int32, (HALF, H), 1)
    for ref, owner in ((send_ref, 1 - core), (keep_ref, core)):
        pick = jnp.where(column == unit + OWN * owner, 1.0, 0.0).astype(bf16)
        ref[...] = lax.dot_general(pick, act, nt, preferred_element_type=f32).astype(bf16)


def error_kernel(arrived_ref, pred_hbm, send_hbm, error_ref, out_ref, pred_ref, send_ref, sems):
    pred_copy = pltpu.make_async_copy(pred_hbm, pred_ref, sems.at[0])
    send_copy = pltpu.make_async_copy(send_hbm, send_ref, sems.at[1])
    pred_copy.start()
    send_copy.start()
    out_ref[:, DW:] = jnp.zeros((HALF, WIDE - DW), bf16)
    live = arrived_ref[:, DW : DW + 1].astype(f32) > 0.5
    target = arrived_ref[:, :DW].astype(f32)
    pred_copy.wait()
    error = jnp.where(live, pred_ref[...] - target, 0.0)
    error = (error / DW).astype(bf16)
    error_ref[...] = error
    send_copy.wait()
    out_ref[:, :DW] = jnp.dot(send_ref[...], error, preferred_element_type=f32).astype(bf16)


def keep_kernel(keep_ref, error_ref, out_ref):
    out_ref[...] = jnp.dot(keep_ref[...], error_ref[...], preferred_element_type=f32)


def add_kernel(own_ref, got_ref, out_ref):
    out_ref[...] = (own_ref[...] + got_ref[:, :DW].astype(f32)).astype(bf16)


def tile_kernel(got_ref, out_ref, sum_ref, flat_ref):
    total = got_ref[0].astype(f32)
    for x in range(1, NX):
        total = total + got_ref[x].astype(f32)
    sum_ref[:, :DW] = total
    sum_ref[:, DW:] = jnp.zeros((XB, WIDE - DW), f32)
    left = lax.broadcasted_iota(jnp.int32, (OWN // 2, 128), 1) < 64
    for y in range(NY):
        at, to = y * OWN, y * TILE_ROWS
        for l in range(4):
            flat_ref[to + l * OWN : to + (l + 1) * OWN, :] = sum_ref[
                at : at + OWN, l * 128 : (l + 1) * 128
            ]
        upper = sum_ref[at : at + OWN // 2, 512:640]
        lower = pltpu.roll(sum_ref[at + OWN // 2 : at + OWN, 512:640], 64, axis=1)
        flat_ref[to + 80 : to + 90, :] = jnp.where(left, upper, lower)
        flat_ref[to + 90 : to + 96, :] = jnp.zeros((6, 128), f32)
        out_ref[y] = flat_ref[to : to + TILE_ROWS, :].astype(out_ref.dtype)


def adam_kernel(tiles_ref, master_ref, one_ref, two_ref, m_out, f_out, s_out, grad_ref, sum_ref):
    total = tiles_ref[0]
    for z in range(1, NZ):
        total = total + tiles_ref[z]
    sum_ref[...] = total
    for l in range(4):
        grad_ref[:, l * 128 : (l + 1) * 128] = sum_ref[l * OWN : (l + 1) * OWN, :]
    last = sum_ref[80:90, :]
    grad_ref[0:10, 512:640] = last
    grad_ref[10:20, 512:640] = pltpu.roll(last, 64, axis=1)
    gradient = grad_ref[:, :DW]
    master = master_ref[...]
    first_new = beta_first * one_ref[...] + (1.0 - beta_first) * gradient
    second_new = beta_second * two_ref[...] + (1.0 - beta_second) * gradient * gradient
    bias_first = 1.0 - beta_first**ADAM_STEP
    bias_second = 1.0 - beta_second**ADAM_STEP
    update_dir = (
        first_new / bias_first / (jnp.sqrt(second_new / bias_second) + adam_epsilon)
        + decay_rate * master
    )
    m_out[...] = master - learn_rate * update_dir
    f_out[...] = first_new
    s_out[...] = second_new


def exchange(x, axis):
    return lax.all_to_all(x, axis, split_axis=0, concat_axis=0, tiled=True)


def body(
    tokens,
    out_proj,
    phi_mean,
    phi_rotate,
    destinations,
    student_hidden,
    adaptor,
    master,
    moment_one,
    moment_two,
):
    shape = jax.ShapeDtypeStruct
    whole, far = pl.BlockSpec(), pl.BlockSpec(memory_space=pltpu.HBM)
    outgoing = call(
        teacher_kernel,
        shape((SLOTS, WIDE), bf16),
        (
            destinations.reshape(1, ROWS),
            phi_mean.reshape(1, DT),
            tokens,
            out_proj,
            phi_rotate.T,
        ),
        specs=[whole, whole, far, far, far],
        vmem=63,
        scratch=(
            pltpu.VMEM((ROWS, DT), bf16),
            pltpu.VMEM((STEPS, DT, CHUNK), bf16),
            pltpu.VMEM((STEPS, DW, CHUNK), bf16),
            pltpu.VMEM((ROWS, WIDE), bf16),
            pltpu.SemaphoreType.DMA,
            pltpu.SemaphoreType.DMA((STEPS,)),
            pltpu.SemaphoreType.DMA((STEPS,)),
        ),
        flops=2 * ROWS * DT * (DT + DW) + 2 * SLOTS * ROWS * WIDE,
        moved=2 * (DT * (DT + DW + ROWS) + SLOTS * WIDE),
    )
    arrived = exchange(outgoing.reshape(NZ, CAP, WIDE), "z").reshape(SLOTS, WIDE)

    activated = jax.nn.gelu(student_hidden.astype(f32), approximate=False).astype(bf16)
    core = lax.axis_index("c").astype(jnp.int32).reshape(1)
    predicted, act_send, act_keep = call(
        student_kernel,
        (shape((SLOTS, DW), f32), shape((HALF, SLOTS), bf16), shape((HALF, SLOTS), bf16)),
        (core, activated, adaptor.T),
        specs=[pl.BlockSpec(memory_space=pltpu.SMEM), whole, whole],
        flops=2 * SLOTS * H * (DW + H),
        moved=2 * SLOTS * H * 2 + 2 * H * DW + 4 * SLOTS * DW,
    )
    error, for_partner = call(
        error_kernel,
        (shape((SLOTS, DW), bf16), shape((HALF, WIDE), bf16)),
        (arrived, predicted, act_send),
        specs=[whole, far, far],
        scratch=(
            pltpu.VMEM((SLOTS, DW), f32),
            pltpu.VMEM((HALF, SLOTS), bf16),
            pltpu.SemaphoreType.DMA((2,)),
        ),
        flops=2 * SLOTS * HALF * DW,
        moved=2 * SLOTS * (WIDE + 3 * DW + HALF) + 2 * HALF * DW,
    )
    from_partner = lax.ppermute(for_partner, "c", [(0, 1), (1, 0)])
    own = call(
        keep_kernel,
        shape((HALF, DW), f32),
        (act_keep, error),
        flops=2 * SLOTS * HALF * DW,
        moved=2 * SLOTS * (DW + HALF) + 4 * HALF * DW,
    )
    chip_sum = call(
        add_kernel, shape((HALF, DW), bf16), (own, from_partner), moved=8 * HALF * DW
    )
    by_x = exchange(chip_sum.reshape(NX, XB, DW), "x")
    tiles = call(
        tile_kernel,
        shape((NY, TILE_ROWS, 128), Y_TYPE),
        (by_x,),
        scratch=(pltpu.VMEM((XB, WIDE), f32), pltpu.VMEM((NY * TILE_ROWS, 128), f32)),
        moved=4 * XB * DW * 4,
    )
    by_y = exchange(tiles, "y")
    part = by_y.astype(f32).sum(axis=0)
    gathered = lax.all_gather(part, "z", axis=0, tiled=False)
    out = shape((OWN, DW), f32)
    return call(
        adam_kernel,
        (out, out, out),
        (gathered, master, moment_one, moment_two),
        scratch=(pltpu.VMEM((OWN, WIDE), f32), pltpu.VMEM((TILE_ROWS, 128), f32)),
        moved=4 * OWN * DW * 7,
    )


def solution(mesh):
    grid = Mesh(mesh.devices.reshape(NZ, NX, NY, NC), ("z", "x", "y", "c"))
    shard = ("x", "y", "c")
    rows = P(("z", "x", "y", "c"), None)
    state = P(shard, None)
    in_specs = (rows, P(), P(), P(), rows, rows, P(), state, state, state)
    return jax.shard_map(
        body, mesh=grid, in_specs=in_specs, out_specs=(state, state, state), check_vma=False
    )
```

```python
import functools

import jax
import jax.numpy as jnp
from jax import lax
from jax.experimental import pallas as pl
from jax.experimental.pallas import tpu as pltpu
from jax.sharding import Mesh, PartitionSpec as P

ADAM_STEP = 1000
beta_first = 0.9
beta_second = 0.999
adam_epsilon = 1e-08
decay_rate = 0.05
learn_rate = 0.001

NZ, NX, NY, NC = 12, 4, 8, 2
CAP = 32
ROWS = 256
SLOTS = NZ * CAP
H = 1280
DW = 576
WIDE = 640
OWN = H // (NX * NY * NC)
HALF = H // NC
XB = HALF // NX
TILE_ROWS = NZ * 8
f32 = jnp.float32
bf16 = jnp.bfloat16
YZ_TYPE = bf16


def call(kernel, outs, args, scratch=(), vmem=24, specs=None, flops=0, moved=0, **kinds):
    return pl.pallas_call(
        kernel,
        out_shape=outs,
        in_specs=specs or [pl.BlockSpec()] * len(args),
        **kinds,
        scratch_shapes=list(scratch),
        compiler_params=pltpu.CompilerParams(vmem_limit_bytes=vmem * 2**20),
        cost_estimate=pl.CostEstimate(flops=flops, bytes_accessed=moved, transcendentals=0),
    )(*args)


def place_kernel(dest_ref, out_ref):
    dest = dest_ref[...]
    spans = lax.broadcasted_iota(jnp.int32, (16, ROWS), 0)
    one_hot = jnp.where(spans == dest, 1.0, 0.0)
    earlier = (
        lax.broadcasted_iota(jnp.int32, (ROWS, ROWS), 0)
        < lax.broadcasted_iota(jnp.int32, (ROWS, ROWS), 1)
    )
    before = jnp.dot(
        one_hot.astype(bf16),
        jnp.where(earlier, 1.0, 0.0).astype(bf16),
        preferred_element_type=f32,
    )
    rank = jnp.sum(before * one_hot, axis=0, keepdims=True)
    slot = dest * CAP + rank.astype(jnp.int32)
    place = lax.broadcasted_iota(jnp.int32, (SLOTS, ROWS), 0) == slot
    out_ref[...] = jnp.where(place, 1.0, 0.0).astype(bf16)


def spread_kernel(place_ref, rows_ref, out_ref):
    place = place_ref[...]
    out_ref[:, :DW] = jnp.dot(place, rows_ref[...], preferred_element_type=f32).astype(bf16)
    live = jnp.sum(place.astype(f32), axis=1, keepdims=True)
    out_ref[:, DW:] = jnp.broadcast_to(live, (SLOTS, WIDE - DW)).astype(bf16)


def student_kernel(core_ref, act_ref, adaptor_t_ref, pred_ref, send_ref, keep_ref):
    nt = (((1,), (1,)), ((), ()))
    act = act_ref[...]
    pred_ref[...] = lax.dot_general(act, adaptor_t_ref[...], nt, preferred_element_type=f32)
    core = core_ref[0]
    place = lax.broadcasted_iota(jnp.int32, (HALF, 1), 0)
    unit = place + OWN * (place // OWN)
    column = lax.broadcasted_iota(jnp.int32, (HALF, H), 1)
    for ref, owner in ((send_ref, 1 - core), (keep_ref, core)):
        pick = jnp.where(column == unit + OWN * owner, 1.0, 0.0).astype(bf16)
        ref[...] = lax.dot_general(pick, act, nt, preferred_element_type=f32).astype(bf16)


def error_kernel(
    arrived_hbm, pred_hbm, send_hbm, error_ref, out_ref, arrived_ref, pred_ref, send_ref, sems
):
    arrived_copy = pltpu.make_async_copy(arrived_hbm, arrived_ref, sems.at[2])
    arrived_copy.start()
    pred_copy = pltpu.make_async_copy(pred_hbm, pred_ref, sems.at[0])
    send_copy = pltpu.make_async_copy(send_hbm, send_ref, sems.at[1])
    pred_copy.start()
    send_copy.start()
    out_ref[:, DW:] = jnp.zeros((HALF, WIDE - DW), bf16)
    arrived_copy.wait()
    live = arrived_ref[:, DW : DW + 1].astype(f32) > 0.5
    target = arrived_ref[:, :DW].astype(f32)
    pred_copy.wait()
    error = jnp.where(live, pred_ref[...] - target, 0.0)
    error = (error / DW).astype(bf16)
    error_ref[...] = error
    send_copy.wait()
    out_ref[:, :DW] = jnp.dot(send_ref[...], error, preferred_element_type=f32).astype(bf16)


def keep_kernel(keep_ref, error_ref, out_ref):
    out_ref[...] = jnp.dot(keep_ref[...], error_ref[...], preferred_element_type=f32)


def add_kernel(own_ref, got_ref, out_ref):
    out_ref[...] = (own_ref[...] + got_ref[:, :DW].astype(f32)).astype(bf16)


def tile_kernel(got_ref, out_ref, sum_ref, flat_ref):
    total = got_ref[0].astype(f32)
    for x in range(1, NX):
        total = total + got_ref[x].astype(f32)
    sum_ref[:, :DW] = total
    sum_ref[:, DW:] = jnp.zeros((XB, WIDE - DW), f32)
    left = lax.broadcasted_iota(jnp.int32, (OWN // 2, 128), 1) < 64
    for y in range(NY):
        at, to = y * OWN, y * TILE_ROWS
        for l in range(4):
            flat_ref[to + l * OWN : to + (l + 1) * OWN, :] = sum_ref[
                at : at + OWN, l * 128 : (l + 1) * 128
            ]
        upper = sum_ref[at : at + OWN // 2, 512:640]
        lower = pltpu.roll(sum_ref[at + OWN // 2 : at + OWN, 512:640], 64, axis=1)
        flat_ref[to + 80 : to + 90, :] = jnp.where(left, upper, lower)
        flat_ref[to + 90 : to + 96, :] = jnp.zeros((6, 128), f32)
        for z in range(NZ):
            out_ref[z * NY + y] = flat_ref[to + z * 8 : to + z * 8 + 8, :].astype(out_ref.dtype)


def adam_kernel(tiles_ref, master_ref, one_ref, two_ref, m_out, f_out, s_out, grad_ref):
    for l in range(4):
        grad_ref[:, l * 128 : (l + 1) * 128] = tiles_ref[l * OWN : (l + 1) * OWN, :]
    last = tiles_ref[80:90, :]
    grad_ref[0:10, 512:640] = last
    grad_ref[10:20, 512:640] = pltpu.roll(last, 64, axis=1)
    gradient = grad_ref[:, :DW]
    master = master_ref[...]
    first_new = beta_first * one_ref[...] + (1.0 - beta_first) * gradient
    second_new = beta_second * two_ref[...] + (1.0 - beta_second) * gradient * gradient
    bias_first = 1.0 - beta_first**ADAM_STEP
    bias_second = 1.0 - beta_second**ADAM_STEP
    update_dir = (
        first_new / bias_first / (jnp.sqrt(second_new / bias_second) + adam_epsilon)
        + decay_rate * master
    )
    m_out[...] = master - learn_rate * update_dir
    f_out[...] = first_new
    s_out[...] = second_new


def exchange(x, axis):
    return lax.all_to_all(x, axis, split_axis=0, concat_axis=0, tiled=True)


def body(
    tokens,
    out_proj,
    phi_mean,
    phi_rotate,
    destinations,
    student_hidden,
    adaptor,
    master,
    moment_one,
    moment_two,
):
    shape = jax.ShapeDtypeStruct
    whole, far = pl.BlockSpec(), pl.BlockSpec(memory_space=pltpu.HBM)
    place = call(place_kernel, shape((SLOTS, ROWS), bf16), (destinations.reshape(1, ROWS),))
    place, tokens = lax.optimization_barrier((place, tokens))
    projected = (jnp.dot(tokens, out_proj, preferred_element_type=f32) - phi_mean).astype(bf16)
    target = jnp.dot(projected, phi_rotate, preferred_element_type=f32).astype(bf16)
    outgoing = call(
        spread_kernel,
        shape((SLOTS, WIDE), bf16),
        (place, target),
        flops=2 * SLOTS * ROWS * WIDE,
        moved=2 * WIDE * (SLOTS + ROWS),
    )
    arrived = exchange(outgoing.reshape(NZ, CAP, WIDE), "z").reshape(SLOTS, WIDE)

    activated = jax.nn.gelu(student_hidden.astype(f32), approximate=False).astype(bf16)
    core = lax.axis_index("c").astype(jnp.int32).reshape(1)
    predicted, act_send, act_keep = call(
        student_kernel,
        (shape((SLOTS, DW), f32), shape((HALF, SLOTS), bf16), shape((HALF, SLOTS), bf16)),
        (core, activated, adaptor.T),
        specs=[pl.BlockSpec(memory_space=pltpu.SMEM), whole, whole],
        flops=2 * SLOTS * H * (DW + H),
        moved=2 * SLOTS * H * 2 + 2 * H * DW + 4 * SLOTS * DW,
    )
    error, for_partner = call(
        error_kernel,
        (shape((SLOTS, DW), bf16), shape((HALF, WIDE), bf16)),
        (arrived, predicted, act_send),
        specs=[far, far, far],
        vmem=60,
        scratch=(
            pltpu.VMEM((SLOTS, WIDE), bf16),
            pltpu.VMEM((SLOTS, DW), f32),
            pltpu.VMEM((HALF, SLOTS), bf16),
            pltpu.SemaphoreType.DMA((3,)),
        ),
        flops=2 * SLOTS * HALF * DW,
        moved=2 * SLOTS * (WIDE + 3 * DW + HALF) + 2 * HALF * DW,
    )
    from_partner = lax.ppermute(for_partner, "c", [(0, 1), (1, 0)])
    own = call(
        keep_kernel,
        shape((HALF, DW), f32),
        (act_keep, error),
        flops=2 * SLOTS * HALF * DW,
        moved=2 * SLOTS * (DW + HALF) + 4 * HALF * DW,
    )
    chip_sum = call(
        add_kernel, shape((HALF, DW), bf16), (own, from_partner), moved=8 * HALF * DW
    )
    by_x = exchange(chip_sum.reshape(NX, XB, DW), "x")
    tiles = call(
        tile_kernel,
        shape((NZ * NY, 8, 128), YZ_TYPE),
        (by_x,),
        scratch=(pltpu.VMEM((XB, WIDE), f32), pltpu.VMEM((NY * TILE_ROWS, 128), f32)),
        moved=4 * XB * DW * 4,
    )
    by_yz = exchange(tiles, ("z", "y"))
    part = by_yz.astype(f32).sum(axis=0)
    gathered = lax.all_gather(part, "z", axis=0, tiled=True)
    out = shape((OWN, DW), f32)
    return call(
        adam_kernel,
        (out, out, out),
        (gathered, master, moment_one, moment_two),
        scratch=(pltpu.VMEM((OWN, WIDE), f32),),
        moved=4 * OWN * DW * 7,
    )


def solution(mesh):
    grid = Mesh(mesh.devices.reshape(NZ, NX, NY, NC), ("z", "x", "y", "c"))
    shard = ("x", "y", "c")
    rows = P(("z", "x", "y", "c"), None)
    state = P(shard, None)
    in_specs = (rows, P(), P(), P(), rows, rows, P(), state, state, state)
    return jax.shard_map(
        body, mesh=grid, in_specs=in_specs, out_specs=(state, state, state), check_vma=False
    )
```

```python
import jax
import jax.numpy as jnp
from jax import lax
from jax.experimental import pallas as pl
from jax.experimental.pallas import tpu as pltpu
from jax.sharding import Mesh, PartitionSpec as P

ADAM_STEP = 1000
beta_first = 0.9
beta_second = 0.999
adam_epsilon = 1e-08
decay_rate = 0.05
learn_rate = 0.001

NZ, NX, NY, NC = 12, 4, 8, 2
CAP = 32
ROWS = 256
SLOTS = NZ * CAP
H = 1280
DW = 576
WIDE = 640
OWN = 20
XB = H // NX
YB = XB // NY
PACKED = 2 * CAP + 8
XROWS = 2 * XB + XB // 4
TILE_ROWS = NZ * 8
EMPTY = 1e30
f32 = jnp.float32
bf16 = jnp.bfloat16
NT = (((1,), (1,)), ((), ()))


def call(kernel, outs, args, scratch=(), vmem=24, specs=None, flops=0, moved=0):
    return pl.pallas_call(
        kernel,
        out_shape=outs,
        in_specs=specs or [pl.BlockSpec()] * len(args),
        scratch_shapes=list(scratch),
        compiler_params=pltpu.CompilerParams(vmem_limit_bytes=vmem * 2**20),
        cost_estimate=pl.CostEstimate(flops=flops, bytes_accessed=moved, transcendentals=0),
    )(*args)


def turn(x, by):
    by = by % 128
    return pltpu.roll(x, by, axis=x.ndim - 1) if by else x


def quarters(parts):
    lane = lax.broadcasted_iota(jnp.int32, parts[0].shape, parts[0].ndim - 1)
    out = parts[3]
    for q in (2, 1, 0):
        out = jnp.where(lane < 32 * (q + 1), parts[q], out)
    return out


def place_kernel(dest_ref, out_ref):
    dest = dest_ref[...]
    spans = lax.broadcasted_iota(jnp.int32, (16, ROWS), 0)
    one_hot = jnp.where(spans == dest, 1.0, 0.0)
    earlier = (
        lax.broadcasted_iota(jnp.int32, (ROWS, ROWS), 0)
        < lax.broadcasted_iota(jnp.int32, (ROWS, ROWS), 1)
    )
    before = jnp.dot(
        one_hot.astype(bf16),
        jnp.where(earlier, 1.0, 0.0).astype(bf16),
        preferred_element_type=f32,
    )
    rank = jnp.sum(before * one_hot, axis=0, keepdims=True)
    slot = dest * CAP + rank.astype(jnp.int32)
    place = lax.broadcasted_iota(jnp.int32, (SLOTS, ROWS), 0) == slot
    out_ref[...] = jnp.where(place, 1.0, 0.0).astype(bf16)


def spread_kernel(place_ref, rows_ref, out_ref, last_ref):
    place = place_ref[...]
    live = jnp.sum(place.astype(f32), axis=1, keepdims=True) > 0.5
    main = jnp.dot(place, rows_ref[:, :512], preferred_element_type=f32)
    main = jnp.where(live, main, EMPTY).astype(bf16)
    last = jnp.dot(place, rows_ref[:, 512:], preferred_element_type=f32)
    last_ref[:, 64:] = jnp.zeros((SLOTS, 64), f32)
    last_ref[:, :64] = jnp.where(live, last, EMPTY)
    last = last_ref[...].reshape(NZ, CAP, 128)
    for c in range(NC):
        packed = quarters(
            [turn(last[:, 8 * q : 8 * q + 8, :], 32 * (q - c)) for q in range(4)]
        ).astype(bf16)
        for z in range(NZ):
            rows = slice(z * CAP, (z + 1) * CAP)
            at = 256 * c
            out_ref[NC * z + c, 0:32, :] = main[rows, at : at + 128]
            out_ref[NC * z + c, 32:64, :] = main[rows, at + 128 : at + 256]
            out_ref[NC * z + c, 64:72, :] = packed[z]


def student_kernel(core_ref, own_ref, other_ref, adaptor_t_ref, pred_ref, last_ref, act_t_ref):
    core = core_ref[0]
    main = adaptor_t_ref[pl.ds(pl.multiple_of(core * 256, 256), 256), :]
    last = adaptor_t_ref[pl.ds(pl.multiple_of(512 + core * 32, 32), 32), :]
    same = lax.broadcasted_iota(jnp.int32, (H, H), 0) == lax.broadcasted_iota(
        jnp.int32, (H, H), 1
    )
    same = jnp.where(same, 1.0, 0.0).astype(bf16)
    for s, ref in enumerate((own_ref, other_ref)):
        rows = slice(s * SLOTS, (s + 1) * SLOTS)
        act = ref[...]
        pred_ref[rows, :] = lax.dot_general(act, main, NT, preferred_element_type=f32)
        last_ref[rows, :] = lax.dot_general(act, last, NT, preferred_element_type=f32)
        act_t_ref[:, rows] = lax.dot_general(same, act, NT, preferred_element_type=f32).astype(
            bf16
        )


def error_kernel(
    core_ref, arrived_ref, pred_ref, last_ref, act_t_ref, out_ref, main_t, last_t, grad_last
):
    core = core_ref[0]
    for s in range(NC):
        source = core if s == 0 else 1 - core
        for z in range(NZ):
            block = arrived_ref[NC * z + source].astype(f32)
            at = s * SLOTS + z * CAP
            main_t[at : at + CAP, 0:128] = block[0:32]
            main_t[at : at + CAP, 128:256] = block[32:64]
            for q in range(4):
                last_t[at + 8 * q : at + 8 * q + 8, :] = turn(block[64:72], -32 * q)

    def scaled(pred, target):
        return (jnp.where(target < 0.1 * EMPTY, pred - target, 0.0) / DW).astype(bf16)

    act_t = act_t_ref[...]
    grad = jnp.dot(
        act_t, scaled(pred_ref[...], main_t[...]), preferred_element_type=f32
    ).astype(bf16)
    grad_last[:, :32] = jnp.dot(
        act_t, scaled(last_ref[...], last_t[:, :32]), preferred_element_type=f32
    )
    for x in range(NX):
        at = x * XB
        out_ref[x, 0:XB, :] = grad[at : at + XB, 0:128]
        out_ref[x, XB : 2 * XB, :] = grad[at : at + XB, 128:256]
        out_ref[x, 2 * XB :, :] = quarters(
            [turn(grad_last[at + 80 * q : at + 80 * q + 80, :], 32 * q) for q in range(4)]
        ).astype(bf16)


def tile_kernel(got_ref, out_ref, sum_ref, flat_ref):
    total = got_ref[0].astype(f32)
    for x in range(1, NX):
        total = total + got_ref[x].astype(f32)
    sum_ref[...] = total
    for y in range(NY):
        to, at = y * TILE_ROWS, y * YB
        flat_ref[to : to + 40, :] = sum_ref[at : at + 40, :]
        flat_ref[to + 40 : to + 80, :] = sum_ref[XB + at : XB + at + 40, :]
        rest = 2 * XB + (y % 2) * 40
        flat_ref[to + 80 : to + 90, :] = quarters(
            [
                turn(sum_ref[rest + 10 * q : rest + 10 * q + 10, :], 32 * (q - y // 2))
                for q in range(4)
            ]
        )
        flat_ref[to + 90 : to + 96, :] = jnp.zeros((6, 128), f32)
        for z in range(NZ):
            out_ref[z * NY + y] = flat_ref[to + z * 8 : to + z * 8 + 8, :].astype(out_ref.dtype)


def adam_kernel(
    core_ref, tiles_ref, master_ref, one_ref, two_ref, m_out, f_out, s_out, grad_ref, flat_ref
):
    first_core = core_ref[0] == 0
    upper, lower = [], []
    for c in range(NC):
        base = c * TILE_ROWS
        for z in range(NZ):
            flat_ref[base + z * 8 : base + z * 8 + 8, :] = tiles_ref[NC * z + c]
        for part in range(2):
            at = base + 40 * part
            to = 256 * c + 128 * part
            grad_ref[:, to : to + 128] = jnp.where(
                first_core, flat_ref[at : at + 20, :], flat_ref[at + 20 : at + 40, :]
            )
        packed = flat_ref[base + 80 : base + 90, :]
        upper.append(jnp.where(first_core, turn(packed, 32 * c), turn(packed, 32 * c - 64)))
        lower.append(jnp.where(first_core, turn(packed, 32 * c - 32), turn(packed, 32 * c - 96)))
    left = lax.broadcasted_iota(jnp.int32, (10, 128), 1) < 32
    grad_ref[0:10, 512:640] = jnp.where(left, upper[0], upper[1])
    grad_ref[10:20, 512:640] = jnp.where(left, lower[0], lower[1])
    gradient = grad_ref[:, :DW]
    master = master_ref[...]
    first_new = beta_first * one_ref[...] + (1.0 - beta_first) * gradient
    second_new = beta_second * two_ref[...] + (1.0 - beta_second) * gradient * gradient
    bias_first = 1.0 - beta_first**ADAM_STEP
    bias_second = 1.0 - beta_second**ADAM_STEP
    update_dir = (
        first_new / bias_first / (jnp.sqrt(second_new / bias_second) + adam_epsilon)
        + decay_rate * master
    )
    m_out[...] = master - learn_rate * update_dir
    f_out[...] = first_new
    s_out[...] = second_new


def exchange(x, axis):
    return lax.all_to_all(x, axis, split_axis=0, concat_axis=0, tiled=True)


def body(
    tokens,
    out_proj,
    phi_mean,
    phi_rotate,
    destinations,
    student_hidden,
    adaptor,
    master,
    moment_one,
    moment_two,
):
    shape = jax.ShapeDtypeStruct
    whole, scalar = pl.BlockSpec(), pl.BlockSpec(memory_space=pltpu.SMEM)
    core = lax.axis_index("c").astype(jnp.int32).reshape(1)
    place = call(place_kernel, shape((SLOTS, ROWS), bf16), (destinations.reshape(1, ROWS),))
    place, tokens = lax.optimization_barrier((place, tokens))
    projected = (jnp.dot(tokens, out_proj, preferred_element_type=f32) - phi_mean).astype(bf16)
    target = jnp.dot(projected, phi_rotate, preferred_element_type=f32).astype(bf16)
    outgoing = call(
        spread_kernel,
        shape((NZ * NC, PACKED, 128), bf16),
        (place, target),
        scratch=(pltpu.VMEM((SLOTS, 128), f32),),
        flops=2 * SLOTS * ROWS * WIDE,
        moved=2 * WIDE * (SLOTS + ROWS),
    )
    arrived = exchange(outgoing, ("z", "c"))
    activated = jax.nn.gelu(student_hidden.astype(f32), approximate=False).astype(bf16)
    other = lax.ppermute(activated, "c", [(0, 1), (1, 0)])
    both = NC * SLOTS
    predicted, predicted_last, act_t = call(
        student_kernel,
        (shape((both, 256), f32), shape((both, 32), f32), shape((H, both), bf16)),
        (core, activated, other, adaptor.T),
        specs=[scalar, whole, whole, whole],
        flops=2 * both * H * (288 + H),
        moved=2 * both * H * 2 + 2 * H * DW + 4 * both * 384,
    )
    partial = call(
        error_kernel,
        shape((NX, XROWS, 128), bf16),
        (core, arrived, predicted, predicted_last, act_t),
        specs=[scalar, whole, whole, whole, whole],
        scratch=(
            pltpu.VMEM((both, 256), f32),
            pltpu.VMEM((both, 128), f32),
            pltpu.VMEM((H, 128), f32),
        ),
        flops=2 * both * H * 384,
        moved=2 * both * H + 4 * both * 384,
    )
    by_x = exchange(partial, "x")
    tiles = call(
        tile_kernel,
        shape((NZ * NY, 8, 128), bf16),
        (by_x,),
        scratch=(pltpu.VMEM((XROWS, 128), f32), pltpu.VMEM((NY * TILE_ROWS, 128), f32)),
        moved=4 * XROWS * 128 * 4,
    )
    by_yz = exchange(tiles, ("z", "y"))
    part = by_yz.astype(f32).sum(axis=0)
    gathered = exchange(jnp.broadcast_to(part, (NZ * NC, 8, 128)), ("z", "c"))
    out = shape((OWN, DW), f32)
    return call(
        adam_kernel,
        (out, out, out),
        (core, gathered, master, moment_one, moment_two),
        specs=[scalar, whole, whole, whole, whole],
        scratch=(pltpu.VMEM((OWN, WIDE), f32), pltpu.VMEM((NC * TILE_ROWS, 128), f32)),
        moved=4 * OWN * DW * 7,
    )


def solution(mesh):
    grid = Mesh(mesh.devices.reshape(NZ, NX, NY, NC), ("z", "x", "y", "c"))
    rows = P(("z", "x", "y", "c"), None)
    state = P(("x", "y", "c"), None)
    in_specs = (rows, P(), P(), P(), rows, rows, P(), state, state, state)
    return jax.shard_map(
        body, mesh=grid, in_specs=in_specs, out_specs=(state, state, state), check_vma=False
    )
```

```python
import jax
import jax.numpy as jnp
from jax import lax
from jax.experimental import pallas as pl
from jax.experimental.pallas import tpu as pltpu
from jax.sharding import Mesh, PartitionSpec as P

ADAM_STEP = 1000
beta_first = 0.9
beta_second = 0.999
adam_epsilon = 1e-08
decay_rate = 0.05
learn_rate = 0.001

NZ, NX, NY, NC = 12, 4, 8, 2
CAP = 32
ROWS = 256
SLOTS = NZ * CAP
H = 1280
DW = 576
WIDE = 640
OWN = 20
XB = H // NX
YB = XB // NY
PACKED = 2 * CAP + 8
XROWS = 2 * XB + XB // 4
TILE_ROWS = NZ * 8
EMPTY = 1e30
f32 = jnp.float32
bf16 = jnp.bfloat16
NT = (((1,), (1,)), ((), ()))


def call(kernel, outs, args, scratch=(), vmem=24, specs=None, flops=0, moved=0):
    return pl.pallas_call(
        kernel,
        out_shape=outs,
        in_specs=specs or [pl.BlockSpec()] * len(args),
        scratch_shapes=list(scratch),
        compiler_params=pltpu.CompilerParams(vmem_limit_bytes=vmem * 2**20),
        cost_estimate=pl.CostEstimate(flops=flops, bytes_accessed=moved, transcendentals=0),
    )(*args)


def turn(x, by):
    by = by % 128
    return pltpu.roll(x, by, axis=x.ndim - 1) if by else x


def quarters(parts):
    lane = lax.broadcasted_iota(jnp.int32, parts[0].shape, parts[0].ndim - 1)
    out = parts[3]
    for q in (2, 1, 0):
        out = jnp.where(lane < 32 * (q + 1), parts[q], out)
    return out


def place_kernel(dest_ref, out_ref):
    dest = dest_ref[...]
    spans = lax.broadcasted_iota(jnp.int32, (16, ROWS), 0)
    one_hot = jnp.where(spans == dest, 1.0, 0.0)
    earlier = (
        lax.broadcasted_iota(jnp.int32, (ROWS, ROWS), 0)
        < lax.broadcasted_iota(jnp.int32, (ROWS, ROWS), 1)
    )
    before = jnp.dot(
        one_hot.astype(bf16),
        jnp.where(earlier, 1.0, 0.0).astype(bf16),
        preferred_element_type=f32,
    )
    rank = jnp.sum(before * one_hot, axis=0, keepdims=True)
    slot = dest * CAP + rank.astype(jnp.int32)
    place = lax.broadcasted_iota(jnp.int32, (SLOTS, ROWS), 0) == slot
    out_ref[...] = jnp.where(place, 1.0, 0.0).astype(bf16)


def spread_kernel(place_ref, rows_ref, out_ref, last_ref):
    place = place_ref[...]
    live = jnp.sum(place.astype(f32), axis=1, keepdims=True) > 0.5
    main = jnp.dot(place, rows_ref[:, :512], preferred_element_type=f32)
    main = jnp.where(live, main, EMPTY).astype(bf16)
    last = jnp.dot(place, rows_ref[:, 512:], preferred_element_type=f32)
    last_ref[:, 64:] = jnp.zeros((SLOTS, 64), f32)
    last_ref[:, :64] = jnp.where(live, last, EMPTY)
    last = last_ref[...].reshape(NZ, CAP, 128)
    for c in range(NC):
        packed = quarters(
            [turn(last[:, 8 * q : 8 * q + 8, :], 32 * (q - c)) for q in range(4)]
        ).astype(bf16)
        for z in range(NZ):
            rows = slice(z * CAP, (z + 1) * CAP)
            at = 256 * c
            out_ref[NC * z + c, 0:32, :] = main[rows, at : at + 128]
            out_ref[NC * z + c, 32:64, :] = main[rows, at + 128 : at + 256]
            out_ref[NC * z + c, 64:72, :] = packed[z]


def student_kernel(core_ref, act_ref, adaptor_t_ref, pred_ref, act_t_ref):
    core = core_ref[0]
    main = adaptor_t_ref[pl.ds(pl.multiple_of(core * 256, 256), 256), :]
    last = adaptor_t_ref[pl.ds(pl.multiple_of(512 + core * 32, 32), 32), :]
    act = act_ref[...]
    pred_ref[:, :256] = lax.dot_general(act, main, NT, preferred_element_type=f32)
    pred_ref[:, 256:] = lax.dot_general(act, last, NT, preferred_element_type=f32)
    act_t_ref[...] = act.T


def error_kernel(
    core_ref,
    arrived_ref,
    own_pred,
    own_act_t,
    other_pred,
    other_act_t,
    out_ref,
    main_t,
    last_t,
    grad_last,
):
    core = core_ref[0]

    def scaled(pred, target):
        return (jnp.where(target < 0.1 * EMPTY, pred - target, 0.0) / DW).astype(bf16)

    grad = rest = None
    for source, pred, act_t in (
        (core, own_pred, own_act_t),
        (1 - core, other_pred, other_act_t),
    ):
        for z in range(NZ):
            block = arrived_ref[NC * z + source].astype(f32)
            at = z * CAP
            main_t[at : at + CAP, 0:128] = block[0:32]
            main_t[at : at + CAP, 128:256] = block[32:64]
            for q in range(4):
                last_t[at + 8 * q : at + 8 * q + 8, :] = turn(block[64:72], -32 * q)
        units = act_t[...]
        main_part = jnp.dot(units, scaled(pred[:, :256], main_t[...]), preferred_element_type=f32)
        last_part = jnp.dot(units, scaled(pred[:, 256:], last_t[:, :32]), preferred_element_type=f32)
        grad = main_part if grad is None else grad + main_part
        rest = last_part if rest is None else rest + last_part
    grad = grad.astype(bf16)
    grad_last[:, :32] = rest
    for x in range(NX):
        at = x * XB
        out_ref[x, 0:XB, :] = grad[at : at + XB, 0:128]
        out_ref[x, XB : 2 * XB, :] = grad[at : at + XB, 128:256]
        out_ref[x, 2 * XB :, :] = quarters(
            [turn(grad_last[at + 80 * q : at + 80 * q + 80, :], 32 * q) for q in range(4)]
        ).astype(bf16)


def tile_kernel(got_ref, out_ref, sum_ref, flat_ref):
    total = got_ref[0].astype(f32)
    for x in range(1, NX):
        total = total + got_ref[x].astype(f32)
    sum_ref[...] = total
    for y in range(NY):
        to, at = y * TILE_ROWS, y * YB
        flat_ref[to : to + 40, :] = sum_ref[at : at + 40, :]
        flat_ref[to + 40 : to + 80, :] = sum_ref[XB + at : XB + at + 40, :]
        rest = 2 * XB + (y % 2) * 40
        flat_ref[to + 80 : to + 90, :] = quarters(
            [
                turn(sum_ref[rest + 10 * q : rest + 10 * q + 10, :], 32 * (q - y // 2))
                for q in range(4)
            ]
        )
        flat_ref[to + 90 : to + 96, :] = jnp.zeros((6, 128), f32)
        for z in range(NZ):
            out_ref[z * NY + y] = flat_ref[to + z * 8 : to + z * 8 + 8, :].astype(out_ref.dtype)


def adam_kernel(
    core_ref, tiles_ref, master_ref, one_ref, two_ref, m_out, f_out, s_out, grad_ref, flat_ref
):
    first_core = core_ref[0] == 0
    upper, lower = [], []
    for c in range(NC):
        base = c * TILE_ROWS
        for z in range(NZ):
            flat_ref[base + z * 8 : base + z * 8 + 8, :] = tiles_ref[NC * z + c]
        for part in range(2):
            at = base + 40 * part
            to = 256 * c + 128 * part
            grad_ref[:, to : to + 128] = jnp.where(
                first_core, flat_ref[at : at + 20, :], flat_ref[at + 20 : at + 40, :]
            )
        packed = flat_ref[base + 80 : base + 90, :]
        upper.append(jnp.where(first_core, turn(packed, 32 * c), turn(packed, 32 * c - 64)))
        lower.append(jnp.where(first_core, turn(packed, 32 * c - 32), turn(packed, 32 * c - 96)))
    left = lax.broadcasted_iota(jnp.int32, (10, 128), 1) < 32
    grad_ref[0:10, 512:640] = jnp.where(left, upper[0], upper[1])
    grad_ref[10:20, 512:640] = jnp.where(left, lower[0], lower[1])
    gradient = grad_ref[:, :DW]
    master = master_ref[...]
    first_new = beta_first * one_ref[...] + (1.0 - beta_first) * gradient
    second_new = beta_second * two_ref[...] + (1.0 - beta_second) * gradient * gradient
    bias_first = 1.0 - beta_first**ADAM_STEP
    bias_second = 1.0 - beta_second**ADAM_STEP
    update_dir = (
        first_new / bias_first / (jnp.sqrt(second_new / bias_second) + adam_epsilon)
        + decay_rate * master
    )
    m_out[...] = master - learn_rate * update_dir
    f_out[...] = first_new
    s_out[...] = second_new


def exchange(x, axis):
    return lax.all_to_all(x, axis, split_axis=0, concat_axis=0, tiled=True)


def body(
    tokens,
    out_proj,
    phi_mean,
    phi_rotate,
    destinations,
    student_hidden,
    adaptor,
    master,
    moment_one,
    moment_two,
):
    shape = jax.ShapeDtypeStruct
    whole, scalar = pl.BlockSpec(), pl.BlockSpec(memory_space=pltpu.SMEM)
    core = lax.axis_index("c").astype(jnp.int32).reshape(1)
    place = call(place_kernel, shape((SLOTS, ROWS), bf16), (destinations.reshape(1, ROWS),))
    place, tokens = lax.optimization_barrier((place, tokens))
    projected = (jnp.dot(tokens, out_proj, preferred_element_type=f32) - phi_mean).astype(bf16)
    target = jnp.dot(projected, phi_rotate, preferred_element_type=f32).astype(bf16)
    outgoing = call(
        spread_kernel,
        shape((NZ * NC, PACKED, 128), bf16),
        (place, target),
        scratch=(pltpu.VMEM((SLOTS, 128), f32),),
        flops=2 * SLOTS * ROWS * WIDE,
        moved=2 * WIDE * (SLOTS + ROWS),
    )
    arrived = exchange(outgoing, ("z", "c"))
    activated = jax.nn.gelu(student_hidden.astype(f32), approximate=False).astype(bf16)
    other = lax.ppermute(activated, "c", [(0, 1), (1, 0)])

    def student(act):
        return call(
            student_kernel,
            (shape((SLOTS, 288), f32), shape((H, SLOTS), bf16)),
            (core, act, adaptor.T),
            specs=[scalar, whole, whole],
            vmem=60,
            flops=2 * SLOTS * H * 288,
            moved=4 * SLOTS * H + 2 * H * DW + 4 * SLOTS * 384,
        )

    partial = call(
        error_kernel,
        shape((NX, XROWS, 128), bf16),
        (core, arrived, *student(activated), *student(other)),
        specs=[scalar] + [whole] * 5,
        vmem=60,
        scratch=(
            pltpu.VMEM((SLOTS, 256), f32),
            pltpu.VMEM((SLOTS, 128), f32),
            pltpu.VMEM((H, 128), f32),
        ),
        flops=4 * SLOTS * H * 384,
        moved=4 * SLOTS * H + 8 * SLOTS * 384,
    )
    by_x = exchange(partial, "x")
    tiles = call(
        tile_kernel,
        shape((NZ * NY, 8, 128), bf16),
        (by_x,),
        scratch=(pltpu.VMEM((XROWS, 128), f32), pltpu.VMEM((NY * TILE_ROWS, 128), f32)),
        moved=4 * XROWS * 128 * 4,
    )
    by_yz = exchange(tiles, ("z", "y"))
    part = by_yz.astype(f32).sum(axis=0)
    gathered = exchange(jnp.broadcast_to(part, (NZ * NC, 8, 128)), ("z", "c"))
    out = shape((OWN, DW), f32)
    return call(
        adam_kernel,
        (out, out, out),
        (core, gathered, master, moment_one, moment_two),
        specs=[scalar, whole, whole, whole, whole],
        scratch=(pltpu.VMEM((OWN, WIDE), f32), pltpu.VMEM((NC * TILE_ROWS, 128), f32)),
        moved=4 * OWN * DW * 7,
    )


def solution(mesh):
    grid = Mesh(mesh.devices.reshape(NZ, NX, NY, NC), ("z", "x", "y", "c"))
    rows = P(("z", "x", "y", "c"), None)
    state = P(("x", "y", "c"), None)
    in_specs = (rows, P(), P(), P(), rows, rows, P(), state, state, state)
    return jax.shard_map(
        body, mesh=grid, in_specs=in_specs, out_specs=(state, state, state), check_vma=False
    )
```

```python
import jax
import jax.numpy as jnp
from jax import lax
from jax.experimental import pallas as pl
from jax.experimental.pallas import tpu as pltpu
from jax.sharding import Mesh, PartitionSpec as P

ADAM_STEP = 1000
beta_first = 0.9
beta_second = 0.999
adam_epsilon = 1e-08
decay_rate = 0.05
learn_rate = 0.001

NZ, NX, NY, NC = 12, 4, 8, 2
CAP = 32
ROWS = 256
SLOTS = NZ * CAP
H = 1280
DW = 576
WIDE = 640
OWN = 20
XB = H // NX
YB = XB // NY
PACKED = 2 * CAP + 8
XROWS = 2 * XB + XB // 4
TILE_ROWS = NZ * 8
EMPTY = 1e30
f32 = jnp.float32
bf16 = jnp.bfloat16
NT = (((1,), (1,)), ((), ()))


def call(kernel, outs, args, scratch=(), vmem=24, specs=None, flops=0, moved=0):
    return pl.pallas_call(
        kernel,
        out_shape=outs,
        in_specs=specs or [pl.BlockSpec()] * len(args),
        scratch_shapes=list(scratch),
        compiler_params=pltpu.CompilerParams(vmem_limit_bytes=vmem * 2**20),
        cost_estimate=pl.CostEstimate(flops=flops, bytes_accessed=moved, transcendentals=0),
    )(*args)


def turn(x, by):
    by = by % 128
    return pltpu.roll(x, by, axis=x.ndim - 1) if by else x


def quarters(parts):
    lane = lax.broadcasted_iota(jnp.int32, parts[0].shape, parts[0].ndim - 1)
    out = parts[3]
    for q in (2, 1, 0):
        out = jnp.where(lane < 32 * (q + 1), parts[q], out)
    return out


def place_kernel(dest_ref, out_ref):
    dest = dest_ref[...]
    spans = lax.broadcasted_iota(jnp.int32, (16, ROWS), 0)
    one_hot = jnp.where(spans == dest, 1.0, 0.0)
    earlier = (
        lax.broadcasted_iota(jnp.int32, (ROWS, ROWS), 0)
        < lax.broadcasted_iota(jnp.int32, (ROWS, ROWS), 1)
    )
    before = jnp.dot(
        one_hot.astype(bf16),
        jnp.where(earlier, 1.0, 0.0).astype(bf16),
        preferred_element_type=f32,
    )
    rank = jnp.sum(before * one_hot, axis=0, keepdims=True)
    slot = dest * CAP + rank.astype(jnp.int32)
    place = lax.broadcasted_iota(jnp.int32, (SLOTS, ROWS), 0) == slot
    out_ref[...] = jnp.where(place, 1.0, 0.0).astype(bf16)


def spread_kernel(place_ref, rows_ref, out_ref, last_ref):
    place = place_ref[...]
    live = jnp.sum(place.astype(f32), axis=1, keepdims=True) > 0.5
    main = jnp.dot(place, rows_ref[:, :512], preferred_element_type=f32)
    main = jnp.where(live, main, EMPTY).astype(bf16)
    last = jnp.dot(place, rows_ref[:, 512:], preferred_element_type=f32)
    last_ref[:, 64:] = jnp.zeros((SLOTS, 64), f32)
    last_ref[:, :64] = jnp.where(live, last, EMPTY)
    last = last_ref[...].reshape(NZ, CAP, 128)
    for c in range(NC):
        packed = quarters(
            [turn(last[:, 8 * q : 8 * q + 8, :], 32 * (q - c)) for q in range(4)]
        ).astype(bf16)
        for z in range(NZ):
            rows = slice(z * CAP, (z + 1) * CAP)
            at = 256 * c
            out_ref[NC * z + c, 0:32, :] = main[rows, at : at + 128]
            out_ref[NC * z + c, 32:64, :] = main[rows, at + 128 : at + 256]
            out_ref[NC * z + c, 64:72, :] = packed[z]


def student_kernel(core_ref, act_ref, adaptor_t_ref, pred_ref, act_t_ref):
    core = core_ref[0]
    main = adaptor_t_ref[pl.ds(pl.multiple_of(core * 256, 256), 256), :]
    last = adaptor_t_ref[pl.ds(pl.multiple_of(512 + core * 32, 32), 32), :]
    act = act_ref[...]
    pred_ref[:, :256] = lax.dot_general(act, main, NT, preferred_element_type=f32)
    pred_ref[:, 256:] = lax.dot_general(act, last, NT, preferred_element_type=f32)
    act_t_ref[...] = act.T


def error_kernel(
    core_ref,
    arrived_hbm,
    own_pred_hbm,
    own_act_hbm,
    other_pred_hbm,
    other_act_hbm,
    out_ref,
    main_t,
    last_t,
    grad_last,
    arrived_ref,
    own_pred,
    own_act_t,
    other_pred,
    other_act_t,
    sems,
):
    core = core_ref[0]
    copies = [
        pltpu.make_async_copy(far, near, sems.at[i])
        for i, (far, near) in enumerate(
            (
                (arrived_hbm, arrived_ref),
                (own_pred_hbm, own_pred),
                (own_act_hbm, own_act_t),
                (other_pred_hbm, other_pred),
                (other_act_hbm, other_act_t),
            )
        )
    ]
    for copy in copies:
        copy.start()
    copies[0].wait()

    def scaled(pred, target):
        return (jnp.where(target < 0.1 * EMPTY, pred - target, 0.0) / DW).astype(bf16)

    grad = rest = None
    for source, pred, act_t in (
        (core, own_pred, own_act_t),
        (1 - core, other_pred, other_act_t),
    ):
        for z in range(NZ):
            block = arrived_ref[NC * z + source].astype(f32)
            at = z * CAP
            main_t[at : at + CAP, 0:128] = block[0:32]
            main_t[at : at + CAP, 128:256] = block[32:64]
            for q in range(4):
                last_t[at + 8 * q : at + 8 * q + 8, :] = turn(block[64:72], -32 * q)
        first = 1 if pred is own_pred else 3
        copies[first].wait()
        copies[first + 1].wait()
        units = act_t[...]
        main_part = jnp.dot(units, scaled(pred[:, :256], main_t[...]), preferred_element_type=f32)
        last_part = jnp.dot(units, scaled(pred[:, 256:], last_t[:, :32]), preferred_element_type=f32)
        grad = main_part if grad is None else grad + main_part
        rest = last_part if rest is None else rest + last_part
    grad = grad.astype(bf16)
    grad_last[:, :32] = rest
    for x in range(NX):
        at = x * XB
        out_ref[x, 0:XB, :] = grad[at : at + XB, 0:128]
        out_ref[x, XB : 2 * XB, :] = grad[at : at + XB, 128:256]
        out_ref[x, 2 * XB :, :] = quarters(
            [turn(grad_last[at + 80 * q : at + 80 * q + 80, :], 32 * q) for q in range(4)]
        ).astype(bf16)


def tile_kernel(got_ref, out_ref, sum_ref, flat_ref):
    total = got_ref[0].astype(f32)
    for x in range(1, NX):
        total = total + got_ref[x].astype(f32)
    sum_ref[...] = total
    for y in range(NY):
        to, at = y * TILE_ROWS, y * YB
        flat_ref[to : to + 40, :] = sum_ref[at : at + 40, :]
        flat_ref[to + 40 : to + 80, :] = sum_ref[XB + at : XB + at + 40, :]
        rest = 2 * XB + (y % 2) * 40
        flat_ref[to + 80 : to + 90, :] = quarters(
            [
                turn(sum_ref[rest + 10 * q : rest + 10 * q + 10, :], 32 * (q - y // 2))
                for q in range(4)
            ]
        )
        flat_ref[to + 90 : to + 96, :] = jnp.zeros((6, 128), f32)
        for z in range(NZ):
            out_ref[z * NY + y] = flat_ref[to + z * 8 : to + z * 8 + 8, :].astype(out_ref.dtype)


def adam_kernel(
    core_ref, tiles_ref, master_ref, one_ref, two_ref, m_out, f_out, s_out, grad_ref, flat_ref
):
    first_core = core_ref[0] == 0
    upper, lower = [], []
    for c in range(NC):
        base = c * TILE_ROWS
        for z in range(NZ):
            flat_ref[base + z * 8 : base + z * 8 + 8, :] = tiles_ref[NC * z + c]
        for part in range(2):
            at = base + 40 * part
            to = 256 * c + 128 * part
            grad_ref[:, to : to + 128] = jnp.where(
                first_core, flat_ref[at : at + 20, :], flat_ref[at + 20 : at + 40, :]
            )
        packed = flat_ref[base + 80 : base + 90, :]
        upper.append(jnp.where(first_core, turn(packed, 32 * c), turn(packed, 32 * c - 64)))
        lower.append(jnp.where(first_core, turn(packed, 32 * c - 32), turn(packed, 32 * c - 96)))
    left = lax.broadcasted_iota(jnp.int32, (10, 128), 1) < 32
    grad_ref[0:10, 512:640] = jnp.where(left, upper[0], upper[1])
    grad_ref[10:20, 512:640] = jnp.where(left, lower[0], lower[1])
    gradient = grad_ref[:, :DW]
    master = master_ref[...]
    first_new = beta_first * one_ref[...] + (1.0 - beta_first) * gradient
    second_new = beta_second * two_ref[...] + (1.0 - beta_second) * gradient * gradient
    bias_first = 1.0 - beta_first**ADAM_STEP
    bias_second = 1.0 - beta_second**ADAM_STEP
    update_dir = (
        first_new / bias_first / (jnp.sqrt(second_new / bias_second) + adam_epsilon)
        + decay_rate * master
    )
    m_out[...] = master - learn_rate * update_dir
    f_out[...] = first_new
    s_out[...] = second_new


def exchange(x, axis):
    return lax.all_to_all(x, axis, split_axis=0, concat_axis=0, tiled=True)


def body(
    tokens,
    out_proj,
    phi_mean,
    phi_rotate,
    destinations,
    student_hidden,
    adaptor,
    master,
    moment_one,
    moment_two,
):
    shape = jax.ShapeDtypeStruct
    whole, scalar = pl.BlockSpec(), pl.BlockSpec(memory_space=pltpu.SMEM)
    core = lax.axis_index("c").astype(jnp.int32).reshape(1)
    place = call(place_kernel, shape((SLOTS, ROWS), bf16), (destinations.reshape(1, ROWS),))
    place, tokens = lax.optimization_barrier((place, tokens))
    projected = (jnp.dot(tokens, out_proj, preferred_element_type=f32) - phi_mean).astype(bf16)
    target = jnp.dot(projected, phi_rotate, preferred_element_type=f32).astype(bf16)
    outgoing = call(
        spread_kernel,
        shape((NZ * NC, PACKED, 128), bf16),
        (place, target),
        scratch=(pltpu.VMEM((SLOTS, 128), f32),),
        flops=2 * SLOTS * ROWS * WIDE,
        moved=2 * WIDE * (SLOTS + ROWS),
    )
    arrived = exchange(outgoing, ("z", "c"))
    activated = jax.nn.gelu(student_hidden.astype(f32), approximate=False).astype(bf16)
    other = lax.ppermute(activated, "c", [(0, 1), (1, 0)])

    def student(act):
        return call(
            student_kernel,
            (shape((SLOTS, 288), f32), shape((H, SLOTS), bf16)),
            (core, act, adaptor.T),
            specs=[scalar, whole, whole],
            vmem=60,
            flops=2 * SLOTS * H * 288,
            moved=4 * SLOTS * H + 2 * H * DW + 4 * SLOTS * 384,
        )

    partial = call(
        error_kernel,
        shape((NX, XROWS, 128), bf16),
        (core, arrived, *student(activated), *student(other)),
        specs=[scalar] + [pl.BlockSpec(memory_space=pltpu.HBM)] * 5,
        vmem=60,
        scratch=(
            pltpu.VMEM((SLOTS, 256), f32),
            pltpu.VMEM((SLOTS, 128), f32),
            pltpu.VMEM((H, 128), f32),
            pltpu.VMEM((NZ * NC, PACKED, 128), bf16),
            pltpu.VMEM((SLOTS, 288), f32),
            pltpu.VMEM((H, SLOTS), bf16),
            pltpu.VMEM((SLOTS, 288), f32),
            pltpu.VMEM((H, SLOTS), bf16),
            pltpu.SemaphoreType.DMA((5,)),
        ),
        flops=4 * SLOTS * H * 384,
        moved=4 * SLOTS * H + 8 * SLOTS * 384,
    )
    by_x = exchange(partial, "x")
    tiles = call(
        tile_kernel,
        shape((NZ * NY, 8, 128), bf16),
        (by_x,),
        scratch=(pltpu.VMEM((XROWS, 128), f32), pltpu.VMEM((NY * TILE_ROWS, 128), f32)),
        moved=4 * XROWS * 128 * 4,
    )
    by_yz = exchange(tiles, ("z", "y"))
    part = by_yz.astype(f32).sum(axis=0)
    gathered = exchange(jnp.broadcast_to(part, (NZ * NC, 8, 128)), ("z", "c"))
    out = shape((OWN, DW), f32)
    return call(
        adam_kernel,
        (out, out, out),
        (core, gathered, master, moment_one, moment_two),
        specs=[scalar, whole, whole, whole, whole],
        scratch=(pltpu.VMEM((OWN, WIDE), f32), pltpu.VMEM((NC * TILE_ROWS, 128), f32)),
        moved=4 * OWN * DW * 7,
    )


def solution(mesh):
    grid = Mesh(mesh.devices.reshape(NZ, NX, NY, NC), ("z", "x", "y", "c"))
    rows = P(("z", "x", "y", "c"), None)
    state = P(("x", "y", "c"), None)
    in_specs = (rows, P(), P(), P(), rows, rows, P(), state, state, state)
    return jax.shard_map(
        body, mesh=grid, in_specs=in_specs, out_specs=(state, state, state), check_vma=False
    )
```
